32 devices in a mesh: dp: 4 (over y, x), expert: 8 (over z, core).
Axes of the slice: x: 2, y: 2, z: 4, core: 2. Of those that a mesh axis runs over, the one named last changes fastest.
Arguments:
- tokens: bfloat16 [5120, 2048], P(('dp', 'expert')), may hold values from -6 to 6
- routes: int32 [5120, 2], P(('dp', 'expert')), may hold values from 0 to 7, all different within a row; in each aligned block of 160 rows (0 to 159, 160 to 319, ...) at most 60 rows name the same one
- route_gains: float32 [5120, 2], P(('dp', 'expert')), may hold values from 0.1 to 1
- cotangent: bfloat16 [5120, 2048], P(('dp', 'expert')), may hold values from -6 to 6
- w_gate: bfloat16 [8, 2048, 768], P('expert'), may hold values from -0.125 to 0.125
- w_up: bfloat16 [8, 2048, 768], P('expert'), may hold values from -0.125 to 0.125
- w_down: bfloat16 [8, 2048, 768], P('expert'), may hold values from -0.21875 to 0.21875
Outputs:
- layer_output: bfloat16 [5120, 2048], P(('dp', 'expert'))
- input_grad: bfloat16 [5120, 2048], P(('dp', 'expert'))
- grad_gate: bfloat16 [8, 2048, 768], P('expert', 'dp')
- grad_up: bfloat16 [8, 2048, 768], P('expert', 'dp')
- grad_down: bfloat16 [8, 2048, 768], P('expert', 'dp')
The draws below stay inside these ranges and needn't reach their ends.
Inputs may be any that keep to these rules, and one draw needn't show every extreme that they name: `routes`: each row names 2 different experts. Within the rows of one device (aligned blocks of 160 rows) no expert is named more than 60 times, and in some device's rows one expert is named exactly 60 times.
All inputs are finite; a program needn't handle non-finite values.
Results may differ from the reference program's by a relative error of at most 0.015.
Values may be sent and summed in bfloat16 or wider, within the bound.
No kernel may reach another device: no remote copies, remote signals or barrier semaphores. Data moves between devices by JAX's collectives and lax.ppermute only.
A program may use at most 128 MiB of HBM per device.

```python
import math
import jax
import jax.numpy as jnp
import numpy as np
from jax import lax

D = 2048
FF = 768
TOP = 2
TOK_DEV = 160
EXPERTS = 8
CAP = 60
TOKENS = 5120
N_DP = 4
N_EXPERT = 8


def strengthened(drawn, stream_key, source, target, blocks, factor):
    owner, partner = [(jnp.arange(drawn.shape[dim]) // (drawn.shape[dim] // blocks)).reshape([-1 if axis == dim else 1 for axis in range(drawn.ndim)]) for dim in (source, target)]
    chosen = jax.random.permutation(stream_key, blocks)[partner]
    strong = (owner == chosen) | (owner == (partner + blocks // 2) % blocks)
    return jnp.where(strong, factor * drawn, drawn)


def block_scale(stream_key, dims, cuts, smallest, high):
    gain = 1.0
    for dim, shards_of in cuts:
        heights = jax.random.uniform(jax.random.fold_in(jax.random.fold_in(stream_key, 6), dim), (shards_of,), jnp.float32, smallest / len(cuts), high / len(cuts))
        gain = gain * jnp.repeat(jnp.exp(heights), dims[dim] // shards_of).reshape((-1,) + (1,) * (len(dims) - 1 - dim))
    return gain


def deal_out(key, own, number, rows, amount, top, most, lean):
    sequence = jax.random.permutation(key, amount)
    heavy_load, usual = shares(amount, rows * top, most, lean, True), shares(amount, rows * top, most, lean, False)
    places = jnp.arange(amount)

    def named(lengths, turn):
        used = int((lengths > 0).sum())
        fixed = max(1, used // 4)
        shifted = fixed + (places - fixed + turn * (used - fixed)) % max(1, amount - fixed)
        return jnp.zeros((amount,), jnp.int32).at[sequence[jnp.where(places < fixed, places, shifted)]].set(jnp.asarray(lengths, jnp.int32))

    lengths = jnp.where(number % 4 == 0, named(heavy_load, number // 4), named(usual, number - number // 4 - 1))
    mixed = jax.random.permutation(jax.random.fold_in(own, 3), amount)
    source_of, receiver = mixed[0:amount // 2 * 2:2], mixed[1:amount // 2 * 2:2]
    margin = jnp.minimum(lengths[source_of] - 1, most - lengths[receiver]) // 2
    margin = jnp.where((source_of == sequence[0]) | (receiver == sequence[0]) | (lengths[receiver] == 0), 0, jnp.maximum(margin, 0))
    shifted = jax.random.randint(jax.random.fold_in(own, 4), (amount // 2,), 0, 1 << 20) % (margin + 1)
    lengths = lengths.at[source_of].add(-shifted).at[receiver].add(shifted)
    items = jnp.searchsorted(jnp.cumsum(lengths), jnp.arange(rows * top), side="right").astype(jnp.int32)
    listing = items.reshape(top, rows).T
    listing = listing[jax.random.permutation(jax.random.fold_in(own, 1), rows)]
    turn = jax.random.randint(jax.random.fold_in(own, 2), (rows, 1), 0, top)
    return jnp.take_along_axis(listing, (jnp.arange(top)[None, :] + turn) % top, axis=1)


def shares(amount, total, limit, slope, full):
    weights = [(1 << 20) // math.isqrt(grade ** slope) + 1 for grade in range(1, amount + 1)]
    largest = limit if full else min(limit, max(-(-total // amount), total * weights[0] // sum(weights)))
    least = 1 if total - largest >= amount - 1 else 0
    holding, spare = [largest] + [least] * (amount - 1), total - largest - least * (amount - 1)
    while spare > 0:
        candidates = [i for i in range(1, amount) if holding[i] < largest] or [i for i in range(1, amount) if holding[i] < limit]
        pool, left = sum([weights[i] for i in candidates]), spare
        for i in candidates:
            addition = min(limit - holding[i], max(1, left * weights[i] // pool), spare)
            holding[i] = holding[i] + addition
            spare = spare - addition
    return np.array(holding)


def noise(key, dims, spread, limit, shards=(), kind=jnp.bfloat16):
    values = spread * jax.random.normal(key, dims, jnp.float32)
    if shards:
        values = values * block_scale(key, dims, shards, -0.22, 0.18)
    return jnp.clip(values, -limit, limit).astype(kind)


def noise_with(own_key, shape, scale, limit, split, heavy, kind=jnp.bfloat16):
    values = scale * jax.random.normal(own_key, shape, jnp.float32)
    if split:
        values = values * block_scale(own_key, shape, split, -0.22, 0.18)
    return jnp.clip(strengthened(values, jax.random.fold_in(own_key, 3), *heavy), -limit, limit).astype(kind)


def setup_inputs(seed: int = 0) -> dict:
    key_list = jax.random.split(jax.random.key(seed), 8)
    tokens = noise(key_list[0], (TOKENS, D), 1.0, 6.0, ((0, 32),))
    routes_keys = jax.random.split(jax.random.fold_in(key_list[1], 1), TOKENS // TOK_DEV)
    routes_turns = jax.random.permutation(jax.random.fold_in(key_list[1], 3), TOKENS // TOK_DEV)
    routes = jax.vmap(lambda own, number: deal_out(jax.random.fold_in(key_list[1], 2), own, number, TOK_DEV, EXPERTS, TOP, CAP, 2))(routes_keys, routes_turns).reshape((TOKENS, TOP))
    route_gains = jnp.clip(jnp.exp(math.log(1.0) - 2.3025851 * jax.random.uniform(key_list[2], (TOKENS, TOP), jnp.float32) ** block_scale(key_list[2], (TOKENS, TOP), ((0, 32),), -0.2, 0.2)), 0.1, 1.0)
    cotangent = noise_with(key_list[3], (TOKENS, D), 1.0, 6.0, ((0, 32),), (0, 1, 32, 2.75))
    w_gate = noise(key_list[4], (EXPERTS, D, FF), D ** -0.5, 0.125, ((0, 8),))
    w_up = noise(key_list[5], (EXPERTS, D, FF), D ** -0.5, 0.125, ((0, 8),))
    w_down = noise(key_list[6], (EXPERTS, D, FF), FF ** -0.5, 0.21875, ((0, 8),))
    return dict(tokens=tokens, routes=routes, route_gains=route_gains, cotangent=cotangent, w_gate=w_gate, w_up=w_up, w_down=w_down)


def slot_targets(route_rows):
    chosen = route_rows.reshape(-1).astype(jnp.int32)
    labels = jnp.arange(EXPERTS, dtype=jnp.int32)
    matches = (chosen[:, None] == labels[None, :]).astype(jnp.int32)
    before = jnp.cumsum(matches, axis=0).astype(jnp.int32) - matches
    position = jnp.sum(before * matches, axis=1).astype(jnp.int32)
    return (chosen * CAP + position).astype(jnp.int32)


def build_buffer(picked, target):
    return jnp.zeros((EXPERTS * CAP, D), jnp.bfloat16).at[target].set(picked)


def round_partial(value):
    return lax.optimization_barrier(value.astype(jnp.bfloat16)).astype(jnp.float32)


def reference(tokens, routes, route_gains, cotangent, w_gate, w_up, w_down):
    gate_full = w_gate.astype(jnp.float32)
    up_full = w_up.astype(jnp.float32)
    down_full = w_down.astype(jnp.float32)
    tok_groups = tokens.reshape(N_DP, N_EXPERT, TOK_DEV, D)
    route_groups = routes.reshape(N_DP, N_EXPERT, TOK_DEV, TOP)
    gain_groups = route_gains.reshape(N_DP, N_EXPERT, TOK_DEV, TOP)
    cot_groups = cotangent.reshape(N_DP, N_EXPERT, TOK_DEV, D)

    def group_pass(carry, group):
        tok_grp, route_grp, gain_grp, cot_grp = group
        targets = jax.vmap(slot_targets)(route_grp)
        picked = jnp.repeat(tok_grp, TOP, axis=1)
        d_out = (gain_grp.reshape(N_EXPERT, TOK_DEV * TOP, 1) * jnp.repeat(cot_grp, TOP, axis=1).astype(jnp.float32)).astype(jnp.bfloat16)
        sent_rows = jax.vmap(build_buffer)(picked, targets)
        sent_cots = jax.vmap(build_buffer)(d_out, targets)

        def arrange(buffer):
            return buffer.reshape(N_EXPERT, EXPERTS, CAP, D).transpose(1, 0, 2, 3).reshape(EXPERTS, N_EXPERT * CAP, D)

        arrived = arrange(sent_rows).astype(jnp.float32)
        arrived_cot = arrange(sent_cots).astype(jnp.float32)
        pre_gate = jnp.einsum("erd,edf->erf", arrived, gate_full)
        pre_up = jnp.einsum("erd,edf->erf", arrived, up_full)
        sigma_gate = jax.nn.sigmoid(pre_gate)
        activated = pre_gate * sigma_gate
        hidden = (activated * pre_up).astype(jnp.bfloat16)
        produced = jnp.einsum("erf,edf->erd", hidden.astype(jnp.float32), down_full).astype(jnp.bfloat16)
        d_hidden = jnp.einsum("erd,edf->erf", arrived_cot, down_full)
        d_gate = (d_hidden * pre_up * (sigma_gate * (1.0 + pre_gate * (1.0 - sigma_gate)))).astype(jnp.bfloat16)
        d_up = (d_hidden * activated).astype(jnp.bfloat16)
        d_pick = (jnp.einsum("erf,edf->erd", d_gate.astype(jnp.float32), gate_full)
                  + jnp.einsum("erf,edf->erd", d_up.astype(jnp.float32), up_full)).astype(jnp.bfloat16)
        part_gate = jnp.einsum("erd,erf->edf", arrived, d_gate.astype(jnp.float32))
        part_up = jnp.einsum("erd,erf->edf", arrived, d_up.astype(jnp.float32))
        part_down = jnp.einsum("erd,erf->edf", arrived_cot, hidden.astype(jnp.float32))
        carry = (carry[0] + round_partial(part_gate), carry[1] + round_partial(part_up), carry[2] + round_partial(part_down))

        def restore(buffer):
            return buffer.reshape(EXPERTS, N_EXPERT, CAP, D).transpose(1, 0, 2, 3).reshape(N_EXPERT, EXPERTS * CAP, D)

        def take_rows(buffer, target):
            return buffer[target]

        back_out = jax.vmap(take_rows)(restore(produced), targets).astype(jnp.float32)
        back_grad = jax.vmap(take_rows)(restore(d_pick), targets).astype(jnp.float32)
        mixed = jnp.sum(gain_grp[..., None] * back_out.reshape(N_EXPERT, TOK_DEV, TOP, D), axis=2).astype(jnp.bfloat16)
        grad_rows = jnp.sum(back_grad.reshape(N_EXPERT, TOK_DEV, TOP, D), axis=2).astype(jnp.bfloat16)
        return carry, (mixed, grad_rows)

    zeros_grad = jnp.zeros((EXPERTS, D, FF), jnp.float32)
    totals, outputs = lax.scan(group_pass, (zeros_grad, zeros_grad, zeros_grad),
                               (tok_groups, route_groups, gain_groups, cot_groups))
    layer_output = outputs[0].reshape(TOKENS, D)
    input_grad = outputs[1].reshape(TOKENS, D)
    return (layer_output, input_grad, totals[0].astype(jnp.bfloat16),
            totals[1].astype(jnp.bfloat16), totals[2].astype(jnp.bfloat16))
```

```python
import functools

import jax
import jax.numpy as jnp
from jax import lax
from jax.experimental import pallas as pl
from jax.experimental.pallas import tpu as pltpu
from jax.sharding import PartitionSpec as P

BF = jnp.bfloat16
F32 = jnp.float32


def tile_of(size, wanted):
    return wanted if size % wanted == 0 else size


def expert_ids(me, n, half, shape, dim):
    place = lax.rem(me, half)
    base = me - place
    d = lax.broadcasted_iota(jnp.int32, shape, dim)
    e = place + d
    e = jnp.where(e >= half, e - half, e)
    return jnp.where(d < half, base + e, -1)


def row_facts(shape, dim, half, cap):
    r = lax.broadcasted_iota(jnp.int32, shape, dim)
    msg = jnp.zeros(shape, jnp.int32)
    for k in range(1, half):
        msg = msg + (r >= k * 2 * cap).astype(jnp.int32)
    q = r - msg * (2 * cap)
    src = (q >= cap).astype(jnp.int32)
    return msg, src, q - src * cap


def pick_rows(facts, me, n, half, cap, source):
    width = facts.shape[1]
    slots = 8 * ((half + 7) // 8)
    route0, route1 = facts[0:1, :], facts[1:2, :]
    ids = expert_ids(me, n, half, (slots, width), 0).astype(F32)
    first = route0 == ids
    member = first | (route1 == ids)
    before = lax.broadcasted_iota(jnp.int32, (width, width), 0)
    after = lax.broadcasted_iota(jnp.int32, (width, width), 1)
    upper = jnp.where(before < after, 1.0, 0.0).astype(BF)
    rank = jnp.dot(jnp.where(member, 1.0, 0.0).astype(BF), upper, preferred_element_type=F32)
    rank = jnp.where(member, rank, -1.0)
    gain = jnp.where(first, facts[2:3, :], facts[3:4, :])
    rows = half * 2 * cap
    msg, src, slot = row_facts((rows, 1), 0, half, cap)
    wide_rank = jnp.full((rows, width), -1.0, F32)
    wide_gain = jnp.zeros((rows, width), F32)
    for d in range(half):
        here = msg == d
        wide_rank = jnp.where(here, rank[d : d + 1, :], wide_rank)
        wide_gain = jnp.where(here, gain[d : d + 1, :], wide_gain)
    wanted = jnp.where(src == source, slot, -2).astype(F32)
    chosen = wide_rank == wanted
    return (
        jnp.where(chosen, 1.0, 0.0).astype(BF),
        jnp.sum(jnp.where(chosen, wide_gain, 0.0), axis=1, keepdims=True),
    )


def select_kernel(n, half, cap, scaled, *refs):
    own_facts, par_facts, own, par = refs[:4]
    outs = refs[4 : 4 + half]
    s_own, s_par, gain = refs[4 + half :]

    @pl.when(pl.program_id(0) == 0)
    def _():
        me = lax.axis_index("expert")
        a, ga = pick_rows(own_facts[...], me, n, half, cap, 0)
        b, gb = pick_rows(par_facts[...], me, n, half, cap, 1)
        s_own[...] = a
        s_par[...] = b
        gain[...] = ga + gb

    y = jnp.dot(s_own[...], own[...], preferred_element_type=F32)
    y = y + jnp.dot(s_par[...], par[...], preferred_element_type=F32)
    if scaled:
        y = y * gain[...]
    y = y.astype(BF)
    for d in range(half):
        outs[d][...] = y[d * 2 * cap : (d + 1) * 2 * cap, :]


def select(own_facts, par_facts, own, par, n, half, cap, scaled):
    rows, width = own.shape
    wt = tile_of(width, 512)
    total = half * 2 * cap
    facts = pl.BlockSpec((4, rows), lambda i: (0, 0))
    block = pl.BlockSpec((rows, wt), lambda i: (0, i))
    return pl.pallas_call(
        functools.partial(select_kernel, n, half, cap, scaled),
        out_shape=[jax.ShapeDtypeStruct((2 * cap, width), BF)] * half,
        grid=(width // wt,),
        in_specs=[facts, facts, block, block],
        out_specs=[pl.BlockSpec((2 * cap, wt), lambda i: (0, i))] * half,
        scratch_shapes=[
            pltpu.VMEM((total, rows), BF),
            pltpu.VMEM((total, rows), BF),
            pltpu.VMEM((total, 1), F32),
        ],
        cost_estimate=pl.CostEstimate(
            flops=4 * total * rows * width,
            bytes_accessed=4 * rows * width + 2 * total * width,
            transcendentals=0,
        ),
        name="select_scaled" if scaled else "select",
    )(own_facts, par_facts, own, par)


def combine_kernel(n, half, cap, source, weighted, *refs):
    facts_ref = refs[0]
    blocks = refs[1 : 1 + half]
    out = refs[1 + half]
    t_first, t_second = refs[2 + half : 4 + half]

    @pl.when(pl.program_id(0) == 0)
    def _():
        me = lax.axis_index("expert")
        facts = facts_ref[...]
        tokens = facts.shape[0]
        slots = 8 * ((half + 7) // 8)
        ids = expert_ids(me, n, half, (tokens, slots), 1).astype(F32)
        first = facts[:, 0:1] == ids
        member = first | (facts[:, 1:2] == ids)
        after = lax.broadcasted_iota(jnp.int32, (tokens, tokens), 0)
        before = lax.broadcasted_iota(jnp.int32, (tokens, tokens), 1)
        lower = jnp.where(before < after, 1.0, 0.0).astype(BF)
        rank = jnp.dot(lower, jnp.where(member, 1.0, 0.0).astype(BF), preferred_element_type=F32)
        rank0 = jnp.where(first, rank, -1.0)
        rank1 = jnp.where(member & ~first, rank, -1.0)
        rows = half * 2 * cap
        msg, src, slot = row_facts((1, rows), 1, half, cap)
        wanted = jnp.where(src == source, slot, -2).astype(F32)
        wide0 = jnp.full((tokens, rows), -1.0, F32)
        wide1 = wide0
        for d in range(half):
            here = msg == d
            wide0 = jnp.where(here, rank0[:, d : d + 1], wide0)
            wide1 = jnp.where(here, rank1[:, d : d + 1], wide1)
        t0 = jnp.where(wide0 == wanted, 1.0, 0.0)
        t1 = jnp.where(wide1 == wanted, 1.0, 0.0)
        if weighted:
            t_first[...] = t0.astype(BF)
            t_second[...] = t1.astype(BF)
        else:
            t_first[...] = (t0 + t1).astype(BF)

    rows = jnp.concatenate([b[...] for b in blocks], axis=0)
    y = jnp.dot(t_first[...], rows, preferred_element_type=F32)
    if weighted:
        z = jnp.dot(t_second[...], rows, preferred_element_type=F32)
        y = facts_ref[:, 2:3] * y + facts_ref[:, 3:4] * z
    out[...] = y.astype(out.dtype)


def combine(facts, blocks, n, half, cap, source, weighted, dtype):
    tokens = facts.shape[0]
    width = blocks[0].shape[1]
    wt = tile_of(width, 512)
    total = half * 2 * cap
    return pl.pallas_call(
        functools.partial(combine_kernel, n, half, cap, source, weighted),
        out_shape=jax.ShapeDtypeStruct((tokens, width), dtype),
        grid=(width // wt,),
        in_specs=[pl.BlockSpec((tokens, 4), lambda i: (0, 0))]
        + [pl.BlockSpec((2 * cap, wt), lambda i: (0, i))] * half,
        out_specs=pl.BlockSpec((tokens, wt), lambda i: (0, i)),
        scratch_shapes=[pltpu.VMEM((tokens, total), BF), pltpu.VMEM((tokens, total), BF)],
        cost_estimate=pl.CostEstimate(
            flops=2 * (1 + weighted) * tokens * total * width,
            bytes_accessed=2 * total * width + 4 * tokens * width,
            transcendentals=0,
        ),
        name="combine_out" if weighted else "combine_grad",
    )(facts, *blocks)


def forward_kernel(half, cap, *refs):
    blocks = refs[:half]
    w_gate, w_up, w_down = refs[half : half + 3]
    outs = refs[half + 3 : 2 * half + 3]
    arrived, hidden, pre_gate, pre_up, total = refs[2 * half + 3 :]
    step = pl.program_id(0)

    @pl.when(step == 0)
    def _():
        for d in range(half):
            arrived[d * 2 * cap : (d + 1) * 2 * cap, :] = blocks[d][...]

    x = arrived[...]
    g = jnp.dot(x, w_gate[...], preferred_element_type=F32)
    u = jnp.dot(x, w_up[...], preferred_element_type=F32)
    pre_gate[...] = g
    pre_up[...] = u
    h = (g * jax.nn.sigmoid(g) * u).astype(BF)
    hidden[...] = h
    part = lax.dot_general(h, w_down[...], (((1,), (1,)), ((), ())), preferred_element_type=F32)

    @pl.when(step == 0)
    def _():
        total[...] = part

    @pl.when(step > 0)
    def _():
        total[...] += part

    @pl.when(step == pl.num_programs(0) - 1)
    def _():
        for d in range(half):
            outs[d][...] = total[d * 2 * cap : (d + 1) * 2 * cap, :].astype(BF)


def forward(blocks, w_gate, w_up, w_down, half, cap):
    width, ff = w_gate.shape
    ft = tile_of(ff, 256)
    rows = half * 2 * cap
    whole = pl.BlockSpec((2 * cap, width), lambda i: (0, 0))
    weight = pl.BlockSpec((width, ft), lambda i: (0, i))
    strip = pl.BlockSpec((rows, ft), lambda i: (0, i))
    outs = pl.pallas_call(
        functools.partial(forward_kernel, half, cap),
        out_shape=[jax.ShapeDtypeStruct((2 * cap, width), BF)] * half
        + [
            jax.ShapeDtypeStruct((rows, width), BF),
            jax.ShapeDtypeStruct((rows, ff), BF),
            jax.ShapeDtypeStruct((rows, ff), F32),
            jax.ShapeDtypeStruct((rows, ff), F32),
        ],
        grid=(ff // ft,),
        in_specs=[whole] * half + [weight] * 3,
        out_specs=[whole] * half
        + [pl.BlockSpec((rows, width), lambda i: (0, 0)), strip, strip, strip],
        scratch_shapes=[pltpu.VMEM((rows, width), F32)],
        cost_estimate=pl.CostEstimate(
            flops=6 * rows * width * ff,
            bytes_accessed=6 * width * ff + 6 * rows * width,
            transcendentals=rows * ff,
        ),
        name="expert_forward",
    )(*blocks, w_gate, w_up, w_down)
    return outs[:half], *outs[half:]


def backward_kernel(half, cap, *refs):
    cot, w_gate, w_up, w_down, pre_gate, pre_up = refs[:6]
    outs = refs[6 : 6 + half]
    d_gate, d_up, total = refs[6 + half :]
    step = pl.program_id(0)
    d_hidden = jnp.dot(cot[...], w_down[...], preferred_element_type=F32)
    g = pre_gate[...]
    sigma = jax.nn.sigmoid(g)
    dg = (d_hidden * pre_up[...] * (sigma * (1.0 + g * (1.0 - sigma)))).astype(BF)
    du = (d_hidden * (g * sigma)).astype(BF)
    d_gate[...] = dg
    d_up[...] = du
    across = (((1,), (1,)), ((), ()))
    part = lax.dot_general(dg, w_gate[...], across, preferred_element_type=F32)
    part = part + lax.dot_general(du, w_up[...], across, preferred_element_type=F32)

    @pl.when(step == 0)
    def _():
        total[...] = part

    @pl.when(step > 0)
    def _():
        total[...] += part

    @pl.when(step == pl.num_programs(0) - 1)
    def _():
        for d in range(half):
            outs[d][...] = total[d * 2 * cap : (d + 1) * 2 * cap, :].astype(BF)


def backward(cot, w_gate, w_up, w_down, pre_gate, pre_up, half, cap):
    width, ff = w_gate.shape
    ft = tile_of(ff, 256)
    rows = half * 2 * cap
    weight = pl.BlockSpec((width, ft), lambda i: (0, i))
    strip = pl.BlockSpec((rows, ft), lambda i: (0, i))
    outs = pl.pallas_call(
        functools.partial(backward_kernel, half, cap),
        out_shape=[jax.ShapeDtypeStruct((2 * cap, width), BF)] * half
        + [jax.ShapeDtypeStruct((rows, ff), BF)] * 2,
        grid=(ff // ft,),
        in_specs=[pl.BlockSpec((rows, width), lambda i: (0, 0))] + [weight] * 3 + [strip] * 2,
        out_specs=[pl.BlockSpec((2 * cap, width), lambda i: (0, 0))] * half + [strip] * 2,
        scratch_shapes=[pltpu.VMEM((rows, width), F32)],
        cost_estimate=pl.CostEstimate(
            flops=6 * rows * width * ff,
            bytes_accessed=6 * width * ff + 4 * rows * width,
            transcendentals=rows * ff,
        ),
        name="expert_backward",
    )(cot, w_gate, w_up, w_down, pre_gate, pre_up)
    return outs[:half], *outs[half:]


def outer_rows(left, right):
    return lax.dot_general(left, right, (((0,), (0,)), ((), ())), preferred_element_type=F32)


def ring_pairs(n, half, d):
    return [(i, i - i % half + (i % half + d) % half) for i in range(n)]


def swap_pairs(size, bit):
    return [(i, i ^ bit) for i in range(size)]


def two_step(left, right, bits):
    me = lax.axis_index("dp")
    step = left.shape[1] // 4
    one, two = bits

    def columns(q):
        return lax.dynamic_slice_in_dim(left, (me ^ q) * step, step, axis=1)

    away = jnp.concatenate([columns(one), columns(one | two)], axis=1)
    home = jnp.concatenate([columns(0), columns(two)], axis=1)
    sent = outer_rows(away, right).astype(BF)
    came = lax.ppermute(sent, "dp", swap_pairs(4, one))
    kept = outer_rows(home, right).astype(BF)
    passed = (kept[step:].astype(F32) + came[step:].astype(F32)).astype(BF)
    last = lax.ppermute(passed, "dp", swap_pairs(4, two))
    return (kept[:step].astype(F32) + came[:step].astype(F32)) + last.astype(F32)


def shards(tokens, routes, route_gains, cotangent, w_gate, w_up, w_down):
    n = lax.axis_size("expert")
    groups = lax.axis_size("dp")
    half = n // 2
    rows, width = tokens.shape
    cap = 3 * rows * routes.shape[1] // (2 * n)
    w_gate, w_up, w_down = w_gate[0], w_up[0], w_down[0]
    across = [(i, (i + half) % n) for i in range(n)]

    def swap(x):
        return lax.ppermute(x, "expert", across)

    def spread(blocks):
        return [blocks[0]] + [
            lax.ppermute(blocks[d], "expert", ring_pairs(n, half, d)) for d in range(1, half)
        ]

    def collect(blocks):
        return [blocks[0]] + [
            lax.ppermute(blocks[d], "expert", ring_pairs(n, half, half - d)) for d in range(1, half)
        ]

    facts = jnp.concatenate([routes.astype(F32), route_gains], axis=1)
    flat = facts.T
    par_flat = swap(flat)
    par_tokens = swap(tokens)
    par_cot = swap(cotangent)
    par_facts = par_flat.T

    blocks = spread(select(flat, par_flat, tokens, par_tokens, n, half, cap, False))
    produced, arrived, hidden, pre_gate, pre_up = forward(blocks, w_gate, w_up, w_down, half, cap)
    cot_blocks = spread(select(flat, par_flat, cotangent, par_cot, n, half, cap, True))

    back = collect(produced)
    far = swap(combine(par_facts, back, n, half, cap, 1, True, BF))
    near = combine(facts, back, n, half, cap, 0, True, F32)
    layer_output = (near + far.astype(F32)).astype(BF)

    arrived_cot = jnp.concatenate(cot_blocks, axis=0)
    d_pick, d_gate, d_up = backward(
        arrived_cot, w_gate, w_up, w_down, pre_gate, pre_up, half, cap
    )
    back = collect(d_pick)
    far = swap(combine(par_facts, back, n, half, cap, 1, False, BF))
    near = combine(facts, back, n, half, cap, 0, False, F32)
    input_grad = (near + far.astype(F32)).astype(BF)

    if groups == 4:
        cut = hidden.shape[1] // 2
        grad_down = jnp.concatenate(
            [
                two_step(arrived_cot, hidden[:, :cut], (1, 2)),
                two_step(arrived_cot, hidden[:, cut:], (2, 1)),
            ],
            axis=1,
        )
        grad_gate = two_step(arrived, d_gate, (1, 2))
        grad_up = two_step(arrived, d_up, (2, 1))
    else:
        grad_down, grad_gate, grad_up = [
            lax.psum_scatter(
                outer_rows(a, b).astype(BF), "dp", scatter_dimension=0, tiled=True
            )
            for a, b in ((arrived_cot, hidden), (arrived, d_gate), (arrived, d_up))
        ]
    return (
        layer_output,
        input_grad,
        grad_gate.astype(BF)[None],
        grad_up.astype(BF)[None],
        grad_down.astype(BF)[None],
    )


def solution(mesh):
    rows = P(("dp", "expert"), None)
    weight = P("expert", None, None)
    grad = P("expert", "dp", None)
    return jax.shard_map(
        shards,
        mesh=mesh,
        in_specs=(rows, rows, rows, rows, weight, weight, weight),
        out_specs=(rows, rows, grad, grad, grad),
        check_vma=False,
    )
```

```python
import functools

import jax
import jax.numpy as jnp
from jax import lax
from jax.experimental import pallas as pl
from jax.experimental.pallas import tpu as pltpu
from jax.sharding import PartitionSpec as P


BF = jnp.bfloat16
F32 = jnp.float32


def tile_of(size, wanted):
    return wanted if size % wanted == 0 else size


def stride_of(cap):
    return 8 * ((cap + 7) // 8)


def message_experts(me, n, half, shape, dim):
    place = lax.rem(me, half)
    base = me - place
    b = lax.broadcasted_iota(jnp.int32, shape, dim)
    far = b >= half
    e = place + jnp.where(far, b - half, b)
    e = jnp.where(e >= half, e - half, e) + jnp.where(far, half - base, base)
    return jnp.where(b < n, e, -1)


def choose_rows(facts, me, n, half, cap):
    width = facts.shape[1]
    slots = 8 * ((n + 7) // 8)
    stride = stride_of(cap)
    route0, route1 = facts[0:1, :], facts[1:2, :]
    ids = message_experts(me, n, half, (slots, width), 0).astype(F32)
    first = route0 == ids
    member = first | (route1 == ids)
    before = lax.broadcasted_iota(jnp.int32, (width, width), 0)
    after = lax.broadcasted_iota(jnp.int32, (width, width), 1)
    upper = jnp.where(before < after, 1.0, 0.0).astype(BF)
    rank = jnp.dot(jnp.where(member, 1.0, 0.0).astype(BF), upper, preferred_element_type=F32)
    rank = jnp.where(member, rank, -1.0)
    gain = jnp.where(first, facts[2:3, :], facts[3:4, :])
    slot = lax.broadcasted_iota(jnp.int32, (stride, width), 0).astype(F32)
    chosen = [slot == rank[b : b + 1, :] for b in range(n)]
    gains = [
        jnp.sum(jnp.where(chosen[b], gain[b : b + 1, :], 0.0), axis=1, keepdims=True)
        for b in range(n)
    ]
    marks = [jnp.where(c, 1.0, 0.0) for c in chosen]
    return jnp.concatenate(marks, axis=0).astype(BF), jnp.concatenate(gains, axis=0)


def write_messages(marks, gain, left, right, outs, cap):
    stride = stride_of(cap)
    y = jnp.dot(marks, left, preferred_element_type=F32)
    z = jnp.dot(marks, right, preferred_element_type=F32)
    if gain is not None:
        y, z = y * gain, z * gain
    for b, out in enumerate(outs):
        r = b * stride
        out[...] = jnp.concatenate([y[r : r + cap], z[r : r + cap]], axis=0).astype(BF)


def select_kernel(n, half, cap, facts, left, right, *refs):
    outs, marks, gain = refs[:n], refs[n], refs[n + 1]

    @pl.when(pl.program_id(0) == 0)
    def _():
        s, g = choose_rows(facts[...], lax.axis_index("expert"), n, half, cap)
        marks[...] = s
        gain[...] = g

    write_messages(marks[...], None, left[...], right[...], outs, cap)


def select_scaled_kernel(cap, marks, gain, left, right, *outs):
    write_messages(marks[...], gain[...], left[...], right[...], outs, cap)


def select(data, facts, marks, gain, n, half, cap):
    rows, width = data.shape
    wt = tile_of(width // 2, 512)
    steps = width // 2 // wt
    total = n * stride_of(cap)

    def fixed(*shape):
        return pl.BlockSpec(shape, lambda i: (0, 0))

    parts = [pl.BlockSpec((rows, wt), lambda i: (0, i)), pl.BlockSpec((rows, wt), lambda i: (0, i + steps))]
    shapes = [jax.ShapeDtypeStruct((2 * cap, width // 2), BF)] * n
    specs = [pl.BlockSpec((2 * cap, wt), lambda i: (0, i))] * n
    cost = pl.CostEstimate(
        flops=2 * total * rows * width, bytes_accessed=2 * (rows + total) * width, transcendentals=0
    )
    if marks is None:
        outs = pl.pallas_call(
            functools.partial(select_kernel, n, half, cap),
            out_shape=shapes
            + [jax.ShapeDtypeStruct((total, rows), BF), jax.ShapeDtypeStruct((total, 1), F32)],
            grid=(steps,),
            in_specs=[fixed(4, rows)] + parts,
            out_specs=specs + [fixed(total, rows), fixed(total, 1)],
            cost_estimate=cost,
            name="select",
        )(facts, data, data)
        return outs[:n], outs[n], outs[n + 1]
    return pl.pallas_call(
        functools.partial(select_scaled_kernel, cap),
        out_shape=shapes,
        grid=(steps,),
        in_specs=[fixed(total, rows), fixed(total, 1)] + parts,
        out_specs=specs,
        cost_estimate=cost,
        name="select_scaled",
    )(marks, gain, data, data)


def put_rows(blocks, out, half, cap):
    stride = stride_of(cap)
    cut = out.shape[1] // 2
    for s in range(2):
        for d in range(half):
            block = blocks[s * half + d][...]
            r = (2 * d + s) * stride
            for side in range(2):
                piece = block[side * cap : (side + 1) * cap]
                if stride > cap:
                    piece = jnp.concatenate([piece, jnp.zeros((stride - cap, cut), BF)], axis=0)
                out[r : r + stride, side * cut : (side + 1) * cut] = piece


def assemble_kernel(half, cap, *refs):
    put_rows(refs[:-1], refs[-1], half, cap)


def assemble(blocks, half, cap):
    width = 2 * blocks[0].shape[1]
    rows = 2 * half * stride_of(cap)
    return pl.pallas_call(
        functools.partial(assemble_kernel, half, cap),
        out_shape=jax.ShapeDtypeStruct((rows, width), BF),
        cost_estimate=pl.CostEstimate(flops=0, bytes_accessed=4 * rows * width, transcendentals=0),
        name="assemble",
    )(*blocks)


def plan_kernel(half, cap, own, par, out):
    me = lax.axis_index("expert")
    tokens = own.shape[0]
    slots = 8 * ((half + 7) // 8)
    after = lax.broadcasted_iota(jnp.int32, (tokens, tokens), 0)
    before = lax.broadcasted_iota(jnp.int32, (tokens, tokens), 1)
    lower = jnp.where(before < after, 1.0, 0.0).astype(BF)
    place = lax.rem(me, half)
    d = lax.broadcasted_iota(jnp.int32, (tokens, slots), 1)
    e = place + d
    e = jnp.where(e >= half, e - half, e) + (me - place)
    ids = jnp.where(d < half, e, -1).astype(F32)
    stride = stride_of(cap)
    rows = half * 2 * stride
    r = lax.broadcasted_iota(jnp.int32, (1, rows), 1)
    msg = jnp.zeros((1, rows), jnp.int32)
    for k in range(1, half):
        msg = msg + (r >= k * 2 * stride).astype(jnp.int32)
    q = r - msg * (2 * stride)
    for source, facts in enumerate((own, par)):
        first = facts[:, 0:1] == ids
        member = first | (facts[:, 1:2] == ids)
        rank = jnp.dot(lower, jnp.where(member, 1.0, 0.0).astype(BF), preferred_element_type=F32)
        slot = q - source * stride
        wanted = jnp.where((slot >= 0) & (slot < cap), slot, -2).astype(F32)
        for k, mine in enumerate((first, member & ~first)):
            mine = jnp.where(mine, rank, -1.0)
            wide = jnp.full((tokens, rows), -1.0, F32)
            for b in range(half):
                wide = jnp.where(msg == b, mine[:, b : b + 1], wide)
            out[2 * source + k] = jnp.where(wide == wanted, 1.0, 0.0).astype(BF)


def plan(facts, par_facts, half, cap):
    tokens = facts.shape[0]
    return pl.pallas_call(
        functools.partial(plan_kernel, half, cap),
        out_shape=jax.ShapeDtypeStruct((4, tokens, half * 2 * stride_of(cap)), BF),
        name="plan",
    )(facts, par_facts)


def combine_kernel(half, weighted, facts, marks, *refs):
    blocks, rest, out = refs[:half], refs[half:-1], refs[-1]
    rows = jnp.concatenate([b[...] for b in blocks], axis=0)
    if weighted:
        y = jnp.dot(marks[0], rows, preferred_element_type=F32)
        z = jnp.dot(marks[1], rows, preferred_element_type=F32)
        y = facts[:, 2:3] * y + facts[:, 3:4] * z
    else:
        y = jnp.dot(marks[0] + marks[1], rows, preferred_element_type=F32)
    for far in rest:
        y = y + far[...].astype(F32)
    out[...] = y.astype(BF)


def combine(facts, marks, source, blocks, weighted, rest=()):
    tokens = facts.shape[0]
    size, width = blocks[0].shape
    half = len(blocks)
    wt = tile_of(width, 1024)
    total = half * size
    strip = pl.BlockSpec((tokens, wt), lambda i: (0, i))
    return pl.pallas_call(
        functools.partial(combine_kernel, half, weighted),
        out_shape=jax.ShapeDtypeStruct((tokens, width), BF),
        grid=(width // wt,),
        in_specs=[
            pl.BlockSpec((tokens, 4), lambda i: (0, 0)),
            pl.BlockSpec((2, tokens, total), lambda i: (source, 0, 0)),
        ]
        + [pl.BlockSpec((size, wt), lambda i: (0, i))] * half
        + [strip] * len(rest),
        out_specs=strip,
        cost_estimate=pl.CostEstimate(
            flops=2 * (1 + weighted) * tokens * total * width,
            bytes_accessed=2 * total * width + 4 * tokens * width,
            transcendentals=0,
        ),
        name="combine_out" if weighted else "combine_grad",
    )(facts, marks, *blocks, *rest)


ACROSS = (((1,), (1,)), ((), ()))


def forward_kernel(half, cap, *refs):
    blocks, refs = refs[: 2 * half], refs[2 * half :]
    w_gate, w_up, w_down = refs[:3]
    outs = refs[3 : 3 + half]
    arrived, hidden, pre_gate, pre_up = refs[3 + half :]
    phase, step = pl.program_id(0), pl.program_id(1)
    depth = w_gate.shape[0]

    @pl.when((phase == 0) & (step == 0))
    def _():
        put_rows(blocks, arrived, half, cap)

    @pl.when(phase == 0)
    def _():
        x = arrived[:, pl.ds(pl.multiple_of(step * depth, depth), depth)]
        g = jnp.dot(x, w_gate[...], preferred_element_type=F32)
        u = jnp.dot(x, w_up[...], preferred_element_type=F32)

        @pl.when(step == 0)
        def _():
            pre_gate[...] = g
            pre_up[...] = u

        @pl.when(step > 0)
        def _():
            pre_gate[...] += g
            pre_up[...] += u

    @pl.when((phase == 1) & (step == 0))
    def _():
        g = pre_gate[...]
        hidden[...] = (g * jax.nn.sigmoid(g) * pre_up[...]).astype(BF)

    @pl.when(phase == 1)
    def _():
        y = lax.dot_general(hidden[...], w_down[...], ACROSS, preferred_element_type=F32)
        size = y.shape[0] // half
        for d in range(half):
            outs[d][...] = y[d * size : (d + 1) * size].astype(BF)


def whole_of(shape):
    return pl.BlockSpec(shape, lambda p, j: (0,) * len(shape))


def forward(blocks, w_gate, w_up, w_down, half, cap):
    width, ff = w_gate.shape
    depth = tile_of(width, 1024)
    last = width // depth - 1
    size = 2 * stride_of(cap)
    rows = half * size
    early = pl.BlockSpec((depth, ff), lambda p, j: (jnp.where(p == 0, j, last), 0))
    late = pl.BlockSpec((depth, ff), lambda p, j: (jnp.where(p == 0, 0, j), 0))
    outs = pl.pallas_call(
        functools.partial(forward_kernel, half, cap),
        out_shape=[jax.ShapeDtypeStruct((size, width), BF)] * half
        + [
            jax.ShapeDtypeStruct((rows, width), BF),
            jax.ShapeDtypeStruct((rows, ff), BF),
            jax.ShapeDtypeStruct((rows, ff), F32),
            jax.ShapeDtypeStruct((rows, ff), F32),
        ],
        grid=(2, last + 1),
        in_specs=[whole_of((2 * cap, width // 2))] * (2 * half) + [early, early, late],
        out_specs=[pl.BlockSpec((size, depth), lambda p, j: (0, jnp.where(p == 0, 0, j)))] * half
        + [whole_of((rows, width)), whole_of((rows, ff)), whole_of((rows, ff)), whole_of((rows, ff))],
        cost_estimate=pl.CostEstimate(
            flops=6 * rows * width * ff,
            bytes_accessed=6 * width * ff + 6 * rows * width,
            transcendentals=rows * ff,
        ),
        name="expert_forward",
    )(*blocks, w_gate, w_up, w_down)
    return outs[:half], *outs[half:]


def backward_kernel(half, *refs):
    cot, w_gate, w_up, w_down, pre_gate, pre_up = refs[:6]
    outs = refs[6 : 6 + half]
    d_gate, d_up, d_hidden = refs[6 + half :]
    phase, step = pl.program_id(0), pl.program_id(1)

    @pl.when(phase == 0)
    def _():
        part = jnp.dot(cot[...], w_down[...], preferred_element_type=F32)

        @pl.when(step == 0)
        def _():
            d_hidden[...] = part

        @pl.when(step > 0)
        def _():
            d_hidden[...] += part

    @pl.when((phase == 1) & (step == 0))
    def _():
        g = pre_gate[...]
        sigma = jax.nn.sigmoid(g)
        dh = d_hidden[...]
        d_gate[...] = (dh * pre_up[...] * (sigma * (1.0 + g * (1.0 - sigma)))).astype(BF)
        d_up[...] = (dh * (g * sigma)).astype(BF)

    @pl.when(phase == 1)
    def _():
        y = lax.dot_general(d_gate[...], w_gate[...], ACROSS, preferred_element_type=F32)
        y = y + lax.dot_general(d_up[...], w_up[...], ACROSS, preferred_element_type=F32)
        size = y.shape[0] // half
        for d in range(half):
            outs[d][...] = y[d * size : (d + 1) * size].astype(BF)


def backward(cot, w_gate, w_up, w_down, pre_gate, pre_up, half):
    width, ff = w_gate.shape
    depth = tile_of(width, 1024)
    last = width // depth - 1
    rows = cot.shape[0]
    size = rows // half
    early = pl.BlockSpec((depth, ff), lambda p, j: (jnp.where(p == 0, j, last), 0))
    late = pl.BlockSpec((depth, ff), lambda p, j: (jnp.where(p == 0, 0, j), 0))
    outs = pl.pallas_call(
        functools.partial(backward_kernel, half),
        out_shape=[jax.ShapeDtypeStruct((size, width), BF)] * half
        + [jax.ShapeDtypeStruct((rows, ff), BF)] * 2,
        grid=(2, last + 1),
        in_specs=[
            pl.BlockSpec((rows, depth), lambda p, j: (0, jnp.where(p == 0, j, last))),
            late,
            late,
            early,
            whole_of((rows, ff)),
            whole_of((rows, ff)),
        ],
        out_specs=[pl.BlockSpec((size, depth), lambda p, j: (0, jnp.where(p == 0, 0, j)))] * half
        + [whole_of((rows, ff))] * 2,
        scratch_shapes=[pltpu.VMEM((rows, ff), F32)],
        cost_estimate=pl.CostEstimate(
            flops=6 * rows * width * ff,
            bytes_accessed=6 * width * ff + 4 * rows * width,
            transcendentals=rows * ff,
        ),
        name="expert_backward",
    )(cot, w_gate, w_up, w_down, pre_gate, pre_up)
    return outs[:half], *outs[half:]


def outer_rows(left, right):
    return lax.dot_general(left, right, (((0,), (0,)), ((), ())), preferred_element_type=F32)


def message_pairs(n, half, b):
    pairs = []
    for i in range(n):
        base, place = i - i % half, (i % half + b) % half
        pairs.append((i, (base if b < half else half - base) + place))
    return pairs


def swap_pairs(size, bit):
    return [(i, i ^ bit) for i in range(size)]


def finish_kernel(steps, *refs):
    parts, out = refs[:-1], refs[-1]
    for k in range(len(parts) // 3):

        @pl.when(pl.program_id(0) // steps == k)
        def _(k=k):
            kept, came, last = parts[3 * k : 3 * k + 3]
            y = kept[...].astype(F32) + came[...].astype(F32) + last[...].astype(F32)
            out[...] = y.astype(BF)[None]


def finish(*parts):
    rows, ff = parts[2].shape
    count = len(parts) // 3
    tile = tile_of(rows, 512)
    steps = rows // tile
    specs = []
    for k in range(count):
        specs += [
            pl.BlockSpec((tile, ff), lambda i, k=k: (jnp.clip(i - k * steps, 0, steps - 1), 0))
        ] * 3
    return pl.pallas_call(
        functools.partial(finish_kernel, steps),
        out_shape=jax.ShapeDtypeStruct((1, count * rows, ff), BF),
        grid=(count * steps,),
        in_specs=specs,
        out_specs=pl.BlockSpec((1, tile, ff), lambda i: (0, i, 0)),
        cost_estimate=pl.CostEstimate(
            flops=2 * count * rows * ff, bytes_accessed=8 * count * rows * ff, transcendentals=0
        ),
        name="finish",
    )(*parts)


def two_step(left, right, bits, part=0, parts=1):
    me = lax.axis_index("dp")
    whole = left.shape[1] // 4
    step = whole // parts
    one, two = bits

    def columns(q):
        return lax.dynamic_slice_in_dim(left, (me ^ q) * whole + part * step, step, axis=1)

    away = jnp.concatenate([columns(one), columns(one | two)], axis=1)
    sent = outer_rows(away, right).astype(BF)
    came = lax.ppermute(sent, "dp", swap_pairs(4, one))
    home = jnp.concatenate([columns(0), columns(two)], axis=1)
    kept = outer_rows(home, right).astype(BF)
    passed = (kept[step:].astype(F32) + came[step:].astype(F32)).astype(BF)
    last = lax.ppermute(passed, "dp", swap_pairs(4, two))
    return kept, came, last


def layer(tokens, routes, route_gains, cotangent, w_gate, w_up, w_down):
    n = lax.axis_size("expert")
    groups = lax.axis_size("dp")
    half = n // 2
    rows, _ = tokens.shape
    cap = 3 * rows * routes.shape[1] // (2 * n)
    w_gate, w_up, w_down = w_gate[0], w_up[0], w_down[0]

    def swap(x):
        return lax.ppermute(x, "expert", [(i, (i + half) % n) for i in range(n)])

    def spread(blocks):
        return [blocks[0]] + [
            lax.ppermute(blocks[b], "expert", message_pairs(n, half, b))
            for b in range(1, n)
        ]

    def collect(blocks):
        return [blocks[0]] + [
            lax.ppermute(blocks[d], "expert", message_pairs(n, half, half - d))
            for d in range(1, half)
        ]

    facts = jnp.concatenate([routes.astype(F32), route_gains], axis=1)
    messages, marks, gain = select(tokens, facts.T, None, None, n, half, cap)
    blocks = spread(messages)
    cot_messages = select(cotangent, None, marks, gain, n, half, cap)
    cot_blocks = spread(cot_messages)
    par_facts = swap(facts)
    where = plan(facts, par_facts, half, cap)

    produced, arrived, hidden, pre_gate, pre_up = forward(blocks, w_gate, w_up, w_down, half, cap)
    back = collect(produced)
    far = swap(combine(par_facts, where, 1, back, True))
    layer_output = combine(facts, where, 0, back, True, (far,))

    arrived_cot = assemble(cot_blocks, half, cap)
    d_pick, d_gate, d_up = backward(arrived_cot, w_gate, w_up, w_down, pre_gate, pre_up, half)
    back = collect(d_pick)
    far = swap(combine(par_facts, where, 1, back, False))
    input_grad = combine(facts, where, 0, back, False, (far,))

    if groups == 4:
        down_a = two_step(arrived_cot, hidden, (1, 2), 0, 2)
        down_b = two_step(arrived_cot, hidden, (2, 1), 1, 2)
        gate = two_step(arrived, d_gate, (1, 2))
        up = two_step(arrived, d_up, (2, 1))
        grad_down = finish(*down_a, *down_b)
        grad_gate = finish(*gate)
        grad_up = finish(*up)
    else:
        grad_down, grad_gate, grad_up = [
            lax.psum_scatter(
                outer_rows(a, b).astype(BF), "dp", scatter_dimension=0, tiled=True
            )[None]
            for a, b in ((arrived_cot, hidden), (arrived, d_gate), (arrived, d_up))
        ]
    return layer_output, input_grad, grad_gate, grad_up, grad_down


def solution(mesh):
    rows = P(("dp", "expert"), None)
    weight = P("expert", None, None)
    grad = P("expert", "dp", None)
    return jax.shard_map(
        layer,
        mesh=mesh,
        in_specs=(rows, rows, rows, rows, weight, weight, weight),
        out_specs=(rows, rows, grad, grad, grad),
        check_vma=False,
    )
```
